256 devices in a mesh: atom: 32 (over y, z_hi, core), sample: 8 (over z_lo, x).
Axes of the slice: x: 4, y: 4, z: 8 (z_hi: 4, z_lo: 2; z = z_hi * 2 + z_lo), core: 2. Of those that a mesh axis runs over, the one named last changes fastest.
Arguments:
- atom_act: bfloat16 [16, 8192, 128], P('sample', 'atom'), may hold values from -3 to 3
- atom_cond: bfloat16 [8192, 128], P('atom'), may hold values from -6 to 6
- ref_pos: float32 [3, 8192], P(None, 'atom'), may hold values from -9 to 9
- atom_token: int32 [8192], P('atom'), may hold values from 0 to 340, never falling along the last dimension, each value on 1 to 48 neighbouring positions
- w_pair_in: float32 [16, 5], replicated, may hold values from -2.5 to 2.5
- w_rel: float32 [16, 9], replicated, may hold values from -6 to 6
- w_cond_pair: bfloat16 [2, 128, 16], replicated, may hold values from -1 to 1
- w_pair_mlp: float32 [3, 16, 16], replicated, may hold values from -1.5 to 1.5
- w_bias: float32 [3, 4, 16], replicated, may hold values from -6 to 6
- w_cond: bfloat16 [3, 128, 768], replicated, may hold values from -0.5 to 0.5
- w_attn: bfloat16 [3, 128, 512], replicated, may hold values from -0.5 to 0.5
- q_bias: float32 [3, 128], replicated, may hold values from -48 to 48
- w_out: bfloat16 [3, 128, 128], replicated, may hold values from -1 to 1
- w_up: bfloat16 [3, 128, 512], replicated, may hold values from -0.5 to 0.5
- w_down: bfloat16 [3, 256, 128], replicated, may hold values from -0.375 to 0.375
Outputs:
- atom_out: bfloat16 [16, 8192, 128], P('sample', 'atom')
The draws below stay inside these ranges and needn't reach their ends.
Inputs may be any that keep to these rules, and one draw needn't show every extreme that they name: `atom_token`: atoms of one token are consecutive and token numbers never fall along the atoms; a token has 1 to 48 atoms.
All inputs are finite; a program needn't handle non-finite values.
Results may differ from the reference program's by a relative error of at most 0.023.
The reference program's roundings to bfloat16 on the way (of `attn_bias`, `modulated`, `queries`, `attn_probs` and `hidden`) count: a program that leaves them out, or rounds other values in their place, can miss the bound.
Values may be sent and summed in bfloat16 or wider, within the bound.
A program may use at most 64 MiB of HBM per device.

```python
import math
import jax
import jax.numpy as jnp
import numpy as np
from jax import lax

C = 128
CP = 16
HEADS = 4
HD = 32
FFH = 256
QW = 32
KW = 128
HALO = 48
LAYERS = 3
REL_CLIP = 4
NREL = 9
MOST_ATOMS = 48
ATOM_DEV = 256
ATOMS = 8192
SAMPLES = 16
TOKENS = 341


def draw_q_bias(key, part):
    return jnp.clip(jax.random.normal(key, (LAYERS, C), jnp.float32), -6.0, 6.0)


def levels(key, dims, split, smallest, largest):
    loudness = 1.0
    for dim, blocks in split:
        steps = jax.random.uniform(jax.random.fold_in(jax.random.fold_in(key, 6), dim), (blocks,), jnp.float32, smallest / len(split), largest / len(split))
        loudness = loudness * jnp.repeat(jnp.exp(steps), dims[dim] // blocks).reshape((-1,) + (1,) * (len(dims) - 1 - dim))
    return loudness


def split_up(number_of, total, most, lean):
    portions = [(1 << 20) // math.isqrt(rank ** lean) + 1 for rank in range(2, number_of + 1)]
    surplus, counts = total - most - (number_of - 1), [1] * (number_of - 1)
    while surplus > 0:
        movable = [i for i in range(number_of - 1) if counts[i] < most]
        mass, budget = sum([portions[i] for i in movable]), surplus
        for i in movable:
            more = min(most - counts[i], max(1, budget * portions[i] // mass), surplus)
            counts[i] = counts[i] + more
            surplus = surplus - more
    return np.array([most] + counts)


def ragged_sizes(key, number_of, total, limit, lean):
    if number_of == 2:
        one = jax.random.randint(key, (), max(1, total - limit), min(limit, total - 1) + 1)
        return jnp.stack([one, total - one])
    tallies = jnp.asarray(split_up(number_of, total, limit, lean), jnp.int32)
    pairs = (number_of - 1) // 2
    source_of, taker = tallies[1:1 + 2 * pairs:2], tallies[2:2 + 2 * pairs:2]
    margin = jnp.minimum(source_of - 1, limit - taker)
    moved = jax.random.randint(jax.random.fold_in(key, 1), (pairs,), 0, 1 << 20) % (margin + 1)
    tallies = tallies.at[1:1 + 2 * pairs:2].set(source_of - moved).at[2:2 + 2 * pairs:2].set(taker + moved)
    return tallies[jax.random.permutation(jax.random.fold_in(key, 2), number_of)]


def scatter_about(own_key, dims, scale, reach, cuts=(), kind=jnp.bfloat16):
    array = scale * jax.random.normal(own_key, dims, jnp.float32)
    if cuts:
        array = array * levels(own_key, dims, cuts, -0.22, 0.18)
    return jnp.clip(array, -reach, reach).astype(kind)


def setup_inputs(seed: int = 0) -> dict:
    seeds = jax.random.split(jax.random.key(seed), 16)
    atom_act = scatter_about(seeds[0], (SAMPLES, ATOMS, C), 0.5, 3.0, ((0, 8), (1, 32)))
    atom_cond = scatter_about(seeds[1], (ATOMS, C), 1.0, 6.0, ((0, 32),))
    ref_pos = scatter_about(seeds[2], (3, ATOMS), 1.5, 9.0, ((1, 32),), jnp.float32)
    atom_token = jnp.searchsorted(jnp.cumsum(ragged_sizes(seeds[3], TOKENS, ATOMS, MOST_ATOMS, 1)), jnp.arange(ATOMS), side="right").astype(jnp.int32)
    w_pair_in = scatter_about(seeds[4], (CP, 5), 5 ** -0.5, 2.5, (), jnp.float32)
    w_rel = scatter_about(seeds[5], (CP, NREL), 1 ** -0.5, 6.0, (), jnp.float32)
    w_cond_pair = scatter_about(seeds[6], (2, C, CP), (C // 4) ** -0.5, 1.0)
    w_pair_mlp = scatter_about(seeds[7], (3, CP, CP), CP ** -0.5, 1.5, (), jnp.float32)
    w_bias = scatter_about(seeds[8], (LAYERS, HEADS, CP), 1 ** -0.5, 6.0, (), jnp.float32)
    w_cond = scatter_about(seeds[9], (LAYERS, C, 6 * C), C ** -0.5, 0.5)
    w_attn = scatter_about(seeds[10], (LAYERS, C, 4 * C), C ** -0.5, 0.5)
    q_bias = draw_q_bias(jax.random.fold_in(seeds[15], 71), 0)
    w_out = scatter_about(seeds[12], (LAYERS, C, C), (C // 4) ** -0.5, 1.0)
    w_up = scatter_about(seeds[13], (LAYERS, C, 2 * FFH), C ** -0.5, 0.5)
    w_down = scatter_about(seeds[14], (LAYERS, FFH, C), FFH ** -0.5, 0.375)
    return dict(atom_act=atom_act, atom_cond=atom_cond, ref_pos=ref_pos, atom_token=atom_token, w_pair_in=w_pair_in, w_rel=w_rel, w_cond_pair=w_cond_pair, w_pair_mlp=w_pair_mlp, w_bias=w_bias, w_cond=w_cond, w_attn=w_attn, q_bias=q_bias, w_out=w_out, w_up=w_up, w_down=w_down)


def layer_norm(values):
    average = lax.optimization_barrier(jnp.mean(values, axis=-1, keepdims=True))
    centered = values - average
    variance = lax.optimization_barrier(jnp.mean(centered * centered, axis=-1, keepdims=True))
    return centered * lax.rsqrt(variance + 1e-05)

def wide_dot(left, right):
    return jnp.dot(left.astype(jnp.float32), right.astype(jnp.float32), preferred_element_type=jnp.float32)

def key_windows(padded, window_count, along):
    shifts = KW // QW
    new_shape = padded.shape[:along] + (window_count + shifts - 1, QW) + padded.shape[along + 1:]
    blocks = padded.reshape(new_shape)
    pieces = [lax.slice_in_dim(blocks, start_at, start_at + window_count, axis=along) for start_at in range(shifts)]
    stacked = jnp.stack(pieces, axis=along + 1)
    return stacked.reshape(padded.shape[:along] + (window_count, KW) + padded.shape[along + 1:])

def pair_bias(query_feats, key_feats, key_valid, w_pair_in, w_rel, w_pair_mlp, w_bias):
    highest = lax.Precision.HIGHEST
    differences = query_feats[0:3][:, :, :, None] - key_feats[0:3][:, :, None, :]
    query_tok = query_feats[3][:, :, None]
    key_tok = key_feats[3][:, None, :]
    same_token = jnp.where((query_tok == key_tok) & key_valid[:, None, :], 1.0, 0.0).astype(jnp.float32)
    inverse = 1.0 / (1.0 + lax.optimization_barrier(jnp.sum(differences * differences, axis=0)))
    token_gap = jnp.clip(key_tok - query_tok, -REL_CLIP, REL_CLIP)
    classes = jnp.arange(NREL, dtype=jnp.float32) - REL_CLIP
    one_hot = jnp.where(token_gap[None] == classes[:, None, None, None], 1.0, 0.0).astype(jnp.float32)
    pair_rep = jnp.einsum('cx,xwqk->cwqk', w_pair_in[:, 0:3], differences, precision=highest) * same_token[None]
    pair_rep = pair_rep + w_pair_in[:, 3][:, None, None, None] * (inverse * same_token)[None]
    pair_rep = pair_rep + w_pair_in[:, 4][:, None, None, None] * same_token[None]
    pair_rep = pair_rep + jnp.einsum('cr,rwqk->cwqk', w_rel, one_hot, precision=highest)
    pair_rep = pair_rep + query_feats[4:][:, :, :, None] + key_feats[4:][:, :, None, :]
    hidden = jax.nn.relu(jnp.einsum('dc,cwqk->dwqk', w_pair_mlp[0], jax.nn.relu(pair_rep), precision=highest))
    hidden = jax.nn.relu(jnp.einsum('dc,cwqk->dwqk', w_pair_mlp[1], hidden, precision=highest))
    pair_rep = pair_rep + jnp.einsum('dc,cwqk->dwqk', w_pair_mlp[2], hidden, precision=highest)
    average = lax.optimization_barrier(jnp.mean(pair_rep, axis=0, keepdims=True))
    centered = pair_rep - average
    variance = lax.optimization_barrier(jnp.mean(centered * centered, axis=0, keepdims=True))
    normed = centered * lax.rsqrt(jnp.maximum(variance, 0.1))
    return jnp.einsum('lhc,cwqk->lwhqk', w_bias, normed, precision=highest).astype(jnp.bfloat16)

def reference(atom_act, atom_cond, ref_pos, atom_token, w_pair_in, w_rel, w_cond_pair, w_pair_mlp, w_bias, w_cond, w_attn, q_bias, w_out, w_up, w_down):
    window_count = ATOMS // QW
    feature_rows = 4 + CP
    tokens = atom_token.astype(jnp.float32)
    active = jax.nn.relu(atom_cond)
    query_cond = wide_dot(active, w_cond_pair[0]).T
    key_cond = wide_dot(active, w_cond_pair[1]).T
    query_table = jnp.concatenate([ref_pos, tokens[None], query_cond], axis=0)
    key_table = jnp.concatenate([ref_pos, tokens[None], key_cond], axis=0)
    key_padded = jnp.pad(key_table, ((0, 0), (HALO, HALO)))
    query_windows = query_table.reshape(feature_rows, window_count, QW)
    key_feature_windows = key_windows(key_padded, window_count, 1)
    position = jnp.arange(window_count)[:, None] * QW - HALO + jnp.arange(KW)[None, :]
    key_valid = (position >= 0) & (position < ATOMS)
    per_group = ATOM_DEV // QW
    groups = window_count // per_group
    query_groups = jnp.moveaxis(query_windows.reshape(feature_rows, groups, per_group, QW), 1, 0)
    key_groups = jnp.moveaxis(key_feature_windows.reshape(feature_rows, groups, per_group, KW), 1, 0)
    valid_groups = key_valid.reshape(groups, per_group, KW)

    def group_bias(group_items):
        return pair_bias(group_items[0], group_items[1], group_items[2], w_pair_in, w_rel, w_pair_mlp, w_bias)
    biases = lax.map(group_bias, (query_groups, key_groups, valid_groups))
    attn_bias = jnp.moveaxis(biases, 0, 1).reshape(LAYERS, window_count, HEADS, QW, KW)
    scale_factor = HD ** (-0.5)

    def run_sample(sample_act):
        residual = sample_act.astype(jnp.float32)
        for layer_index in range(LAYERS):
            cond_values = wide_dot(atom_cond, w_cond[layer_index])
            modulated = (jax.nn.sigmoid(cond_values[:, 0:C]) * layer_norm(residual) + cond_values[:, C:2 * C]).astype(jnp.bfloat16)
            projected = wide_dot(modulated, w_attn[layer_index])
            queries = (projected[:, 0:C] + q_bias[layer_index]).astype(jnp.bfloat16)
            keyval = projected[:, C:3 * C].astype(jnp.bfloat16)
            gating = jax.nn.sigmoid(projected[:, 3 * C:4 * C])
            keyval_windows = key_windows(jnp.pad(keyval, ((HALO, HALO), (0, 0))), window_count, 0)
            query_heads = queries.reshape(window_count, QW, HEADS, HD).astype(jnp.float32)
            key_heads = keyval_windows[:, :, 0:C].reshape(window_count, KW, HEADS, HD).astype(jnp.float32)
            value_heads = keyval_windows[:, :, C:2 * C].reshape(window_count, KW, HEADS, HD).astype(jnp.float32)
            scores = jnp.einsum('wqhd,wkhd->whqk', query_heads, key_heads) * scale_factor + attn_bias[layer_index].astype(jnp.float32)
            scores = jnp.where(key_valid[:, None, None, :], scores, -jnp.inf)
            row_max = lax.optimization_barrier(jnp.max(scores, axis=-1, keepdims=True))
            exponent = jnp.exp(scores - row_max)
            attn_probs = (exponent / lax.optimization_barrier(jnp.sum(exponent, axis=-1, keepdims=True))).astype(jnp.bfloat16)
            mixed_out = jnp.einsum('whqk,wkhd->wqhd', attn_probs.astype(jnp.float32), value_heads).reshape(ATOMS, C)
            mixed_out = (mixed_out * gating).astype(jnp.bfloat16)
            residual = residual + jax.nn.sigmoid(cond_values[:, 2 * C:3 * C]) * wide_dot(mixed_out, w_out[layer_index])
            modulated2 = (jax.nn.sigmoid(cond_values[:, 3 * C:4 * C]) * layer_norm(residual) + cond_values[:, 4 * C:5 * C]).astype(jnp.bfloat16)
            up_values = wide_dot(modulated2, w_up[layer_index])
            hidden = (jax.nn.silu(up_values[:, 0:FFH]) * up_values[:, FFH:2 * FFH]).astype(jnp.bfloat16)
            residual = residual + jax.nn.sigmoid(cond_values[:, 5 * C:6 * C]) * wide_dot(hidden, w_down[layer_index])
        return residual.astype(jnp.bfloat16)
    return lax.map(run_sample, atom_act)
```

```python
import functools

import jax
import jax.numpy as jnp
from jax import lax
from jax.experimental import pallas as pl
from jax.experimental.pallas import tpu as pltpu
from jax.sharding import PartitionSpec as P

F32 = jnp.float32
BF16 = jnp.bfloat16
MESH = pl.DeviceIdType.MESH

S = 2
A = 256
C = 128
HEADS = 4
HD = 32
FFH = 256
CP = 16
QW = 32
HALO = 48
LAYERS = 3
EXT = A + 2 * HALO
LOG2E = 1.4426950408889634
SCALE = HD**-0.5
NEG = -1e30
WINDOWS = ((0, 1, 6, 7), (2, 3, 4, 5))
SEGMENTS = (((0, 0, 64), (64, 192, 64)), ((0, 64, 128),))


def dot(a, b):
    return lax.dot_general(a, b, (((1,), (0,)), ((), ())), preferred_element_type=F32)


def dot_nt(a, b):
    return lax.dot_general(a, b, (((1,), (1,)), ((), ())), preferred_element_type=F32)


def sigmoid(x):
    return 0.5 * jnp.tanh(0.5 * x) + 0.5


def layer_norm(x):
    mean = jnp.mean(x, axis=-1, keepdims=True)
    xc = x - mean
    var = jnp.mean(xc * xc, axis=-1, keepdims=True)
    return xc * lax.rsqrt(var + 1e-05)


def iota(shape, dim):
    return lax.broadcasted_iota(jnp.int32, shape, dim)


def spread(rows, cols):
    return jnp.where(iota((rows, cols), 0) // 16 == iota((rows, cols), 1), 1.0, 0.0).astype(BF16)


def kron16(m, e_rows, e_cols):
    wide = dot(e_rows, m.astype(BF16)).astype(BF16)
    full = dot_nt(wide, e_cols)
    same = iota(full.shape, 0) % 16 == iota(full.shape, 1) % 16
    return jnp.where(same, full, 0.0)


def kernel(
    act_h, cond_h, pos_h, tok_h, wpi_h, wrel_h, wcp_h, wmlp_h, wb_h, wcond_h, wattn_h, qb_h,
    wout_h, wup_h, wdown_h, out_ref,
    act, cext, t3, tk, wpi, wrel, wcp, wmlp, wb, wcond, wattn, qb, wout, wup, wdown,
    cv, res, qs, gs, mix, kv, bias, emb, cm, km, wbk, qt, qcp, kt, kc,
    lsem, ssem, rsem,
):
    atom = lax.axis_index("atom")
    natom = lax.axis_size("atom")
    right = lax.rem(atom + 1, natom)
    left = lax.rem(atom + natom - 1, natom)

    barrier = pltpu.get_barrier_semaphore()
    for nb in (left, right):
        pl.semaphore_signal(barrier, inc=1, device_id={"atom": nb}, device_id_type=MESH)

    local = []
    for i, (src, dst) in enumerate(
        (
            (act_h, act),
            (cond_h, cext.at[HALO : HALO + A]),
            (wcond_h.at[0], wcond.at[0]),
            (wattn_h, wattn),
            (qb_h, qb),
            (pos_h, t3.at[:, A : 2 * A]),
            (tok_h, tk.at[:, A : 2 * A]),
            (wpi_h, wpi),
            (wrel_h, wrel),
            (wcp_h, wcp),
            (wmlp_h, wmlp),
            (wb_h, wb),
            (wcond_h.at[1:3], wcond.at[1:3]),
            (wout_h, wout),
            (wup_h, wup),
            (wdown_h, wdown),
        )
    ):
        copy = pltpu.make_async_copy(src, dst, lsem.at[i])
        copy.start()
        local.append(copy)

    remote = []

    def send(src, dst, index, to):
        copy = pltpu.make_async_remote_copy(
            src_ref=src,
            dst_ref=dst,
            send_sem=ssem.at[index],
            recv_sem=rsem.at[index],
            device_id={"atom": to},
            device_id_type=MESH,
        )
        copy.start()
        remote.append(copy)

    def send_kv(layer):
        send(kv.at[layer, :, A : A + HALO], kv.at[layer, :, 0:HALO], 2 * layer, right)
        send(kv.at[layer, :, HALO : 2 * HALO], kv.at[layer, :, HALO + A : EXT], 2 * layer + 1, left)

    def cond_rows(group):
        return [cext[HALO + a0 : HALO + a0 + n] for _, a0, n in SEGMENTS[group]]

    def cond_values(layer):
        cond = jnp.concatenate(cond_rows(0) + cond_rows(1), axis=0)
        for part in range(6):
            vals = dot(cond, wcond[layer, :, part * C : (part + 1) * C])
            cv[layer, part] = vals if part in (1, 4) else sigmoid(vals)

    def project(layer, group):
        rows = slice(group * 128, group * 128 + 128)
        mods = []
        for s in range(S):
            mods.append(
                (cv[layer, 0, rows] * layer_norm(res[group, s]) + cv[layer, 1, rows]).astype(BF16)
            )
        mod = jnp.concatenate(mods, axis=0)
        q = dot(mod, wattn[layer, :, 0:C]) + qb[layer : layer + 1, :]
        qs[group] = q.astype(BF16).reshape(S, 128, C)
        keyval = dot(mod, wattn[layer, :, C : 3 * C]).astype(BF16)
        for s in range(S):
            for r0, a0, n in SEGMENTS[group]:
                kv[layer, s, HALO + a0 : HALO + a0 + n] = keyval[s * 128 + r0 : s * 128 + r0 + n]
        gate = dot(mod, wattn[layer, :, 3 * C : 4 * C])
        gs[group] = sigmoid(gate).reshape(S, 128, C)

    lane = iota((QW, C), 1)
    head_masks = [jnp.where(lane // HD == h, 1.0, 0.0).astype(BF16) for h in range(HEADS)]
    ones = jnp.ones((C, C), BF16)

    def by_head(x, c0):
        parts = [x[h * QW : (h + 1) * QW, c0 : c0 + C] for h in range(HEADS)]
        out = parts[HEADS - 1]
        for h in range(HEADS - 2, -1, -1):
            out = jnp.where(lane < (h + 1) * HD, parts[h], out)
        return out

    def attend(layer, group):
        for j in range(4):
            w = WINDOWS[group][j]
            for s in range(S):
                q = qs[group, s, j * QW : (j + 1) * QW]
                big = jnp.concatenate([q * m for m in head_masks], axis=0)
                k = kv[layer, s, w * QW : w * QW + C, 0:C]
                v = kv[layer, s, w * QW : w * QW + C, C : 2 * C]
                t = dot_nt(big, k) * (SCALE * LOG2E) + bias[layer, group, j]
                top = jnp.max(t, axis=-1, keepdims=True)
                e = jnp.exp2(t - top).astype(BF16)
                o = dot(e, jnp.concatenate([v, ones], axis=1))
                mixed = by_head(o, 0) / by_head(o, C) * gs[group, s, j * QW : (j + 1) * QW]
                mix[group, s, j * QW : (j + 1) * QW] = mixed.astype(BF16)

    def transition(layer, group):
        rows = slice(group * 128, group * 128 + 128)
        attended = dot(mix[group].reshape(S * 128, C), wout[layer])
        mods = []
        for s in range(S):
            r = res[group, s] + cv[layer, 2, rows] * attended[s * 128 : (s + 1) * 128]
            res[group, s] = r
            mods.append((cv[layer, 3, rows] * layer_norm(r) + cv[layer, 4, rows]).astype(BF16))
        mod = jnp.concatenate(mods, axis=0)
        up = dot(mod, wup[layer, :, 0:FFH])
        hidden = (up * sigmoid(up) * dot(mod, wup[layer, :, FFH : 2 * FFH])).astype(BF16)
        down = dot(hidden, wdown[layer])
        for s in range(S):
            r = res[group, s] + cv[layer, 5, rows] * down[s * 128 : (s + 1) * 128]
            if layer < LAYERS - 1:
                res[group, s] = r
            else:
                for r0, a0, n in SEGMENTS[group]:
                    out_ref[s, a0 : a0 + n] = r[r0 : r0 + n].astype(BF16)

    def pair_constants():
        e16 = spread(256, 16)
        r16 = iota((16, 16), 0)
        c16 = iota((16, 16), 1)
        place = jnp.where(c16 == jnp.where(r16 < 4, r16, 8), 1.0, 0.0)
        shift = jnp.where(c16 == r16 + 4, 1.0, 0.0)
        weights = lax.dot_general(
            wpi[...], place[0:5], (((1,), (0,)), ((), ())),
            precision=lax.Precision.HIGHEST, preferred_element_type=F32,
        ) + lax.dot_general(
            wrel[...], shift[0:9], (((1,), (0,)), ((), ())),
            precision=lax.Precision.HIGHEST, preferred_element_type=F32,
        )
        base = kron16(weights, e16, e16)
        row = iota((256, 256), 0)
        col = iota((256, 256), 1)
        keyed = (col >= 208) & (col < 240) & (row // 16 == col % 16)
        emb[...] = jnp.where(keyed, 1.0, jnp.where(col < 208, base, 0.0)).astype(BF16)
        cm[...] = jnp.where(
            iota((256, C), 1) == 112 + iota((256, C), 0) // 16, 1.0, 0.0
        ).astype(BF16)
        for i in range(3):
            km[i] = kron16(wmlp[i], e16, e16).astype(BF16)
        e4 = spread(64, HEADS)
        for layer in range(LAYERS):
            wbk[layer * 64 : (layer + 1) * 64] = kron16(wb[layer], e4, e16).astype(BF16)

    def query_tables():
        pos = jnp.concatenate(
            [t3[:, A : 2 * A], tk[:, A : 2 * A].astype(F32), jnp.zeros((124, A), F32)], axis=0
        )
        cols = pos.T
        off = 0
        for group in range(2):
            for _, a0, n in SEGMENTS[group]:
                qt[off : off + n] = cols[a0 : a0 + n]
                off += n
        place = jnp.where(iota((16, C), 1) == 112 + iota((16, C), 0), 1.0, 0.0).astype(BF16)
        w0 = dot(wcp[0], place).astype(BF16)
        cond = jnp.concatenate(cond_rows(0) + cond_rows(1), axis=0)
        qcp[...] = dot(jnp.maximum(cond, 0), w0).astype(BF16)

    def key_tables(group):
        eye = jnp.where(iota((16, 16), 0) == iota((16, 16), 1), 1.0, 0.0).astype(BF16)
        w1 = dot_nt(eye, wcp[1]).astype(BF16)
        for j in range(4):
            w = WINDOWS[group][j]
            cond = jnp.maximum(cext[w * QW : w * QW + C], 0)
            full = dot_nt(w1, cond)
            hi = full.astype(BF16)
            kc[group, j, 0:16] = hi
            kc[group, j, 16:32] = (full - hi.astype(F32)).astype(BF16)
            first = A - HALO + w * QW
            a0 = first // 128 * 128
            wide = jnp.concatenate(
                [t3[:, a0 : a0 + 256], tk[:, a0 : a0 + 256].astype(F32), jnp.zeros((4, 256), F32)],
                axis=0,
            )
            if first > a0:
                wide = pltpu.roll(wide, 256 - (first - a0), 1)
            kt[group, j] = wide[:, 0:C]

    def bias_unit(group, jp, half):
        feats = []
        for i in range(2):
            j = 2 * jp + i
            q0 = pl.multiple_of(group * 128 + j * QW + half * 16, 16)
            qcols = qt[pl.ds(q0, 16), :]
            keys = kt[group, j]
            d = [qcols[:, x : x + 1] - keys[x : x + 1, :] for x in range(3)]
            inv = 1.0 / (1.0 + (d[0] * d[0] + d[1] * d[1] + d[2] * d[2]))
            gap = jnp.clip(keys[3:4, :] - qcols[:, 3:4], -4.0, 4.0)
            hot = [jnp.where(gap == float(g), 1.0, 0.0) for g in range(-4, 5)]
            v = hot[4]
            rows = [v * x for x in d] + [v * inv] + hot
            rhs = jnp.concatenate(
                [x.astype(BF16) for x in rows] + [kc[group, j], jnp.ones((16, C), BF16)], axis=0
            )
            qc = qcp[pl.ds(q0, 16), :]
            tail = emb[:, C : 2 * C] + cm[...] * jnp.concatenate([qc] * 16, axis=0)
            lhs = jnp.concatenate([emb[:, 0:C], tail], axis=1)
            feats.append(dot(lhs, rhs))
        pair = jnp.concatenate(feats, axis=1)
        h = jnp.maximum(dot(km[0], jnp.maximum(pair, 0.0).astype(BF16)), 0.0).astype(BF16)
        h = jnp.maximum(dot(km[1], h), 0.0).astype(BF16)
        pair = (pair + dot(km[2], h)).reshape(CP, 16, 256)
        mean = jnp.sum(pair, axis=0) * (1.0 / CP)
        centered = pair - mean[None]
        var = jnp.sum(centered * centered, axis=0) * (1.0 / CP)
        normed = (centered * lax.rsqrt(jnp.maximum(var, 0.1))[None]).astype(BF16)
        out = dot(wbk[...], normed.reshape(256, 256))
        for i in range(2):
            j = 2 * jp + i
            w = jnp.where(group == 0, jnp.where(j < 2, j, j + 4), j + 2)
            at = atom * A + w * QW - HALO + iota((1, C), 1)
            mask = jnp.where((at >= 0) & (at < natom * A), 0.0, NEG)
            part = out[:, i * C : (i + 1) * C].astype(BF16).astype(F32) * LOG2E + mask
            for layer in range(LAYERS):
                for h in range(HEADS):
                    r0 = layer * 64 + h * 16
                    bias[layer, group, j, pl.ds(h * QW + half * 16, 16), :] = part[r0 : r0 + 16]

    def pair_bias(group):
        @pl.loop(0, 2)
        def _(jp):
            for half in range(2):
                bias_unit(group, jp, half)

    def wait(*which):
        for i in which:
            local[i].wait()

    wait(0, 1, 2, 3, 4)
    for group in range(2):
        for s in range(S):
            for r0, a0, n in SEGMENTS[group]:
                res[group, s, r0 : r0 + n] = act[s, a0 : a0 + n].astype(F32)
    cond_values(0)
    project(0, 0)
    pl.semaphore_wait(barrier, 2)
    send(cond_h.at[A - HALO : A], cext.at[0:HALO], 6, right)
    send(cond_h.at[0:HALO], cext.at[HALO + A : EXT], 7, left)
    send(pos_h, t3.at[:, 0:A], 8, right)
    send(pos_h, t3.at[:, 2 * A : 3 * A], 9, left)
    send(tok_h, tk.at[:, 0:A], 10, right)
    send(tok_h, tk.at[:, 2 * A : 3 * A], 11, left)
    send_kv(0)
    project(0, 1)
    wait(5, 6, 7, 8, 9, 10, 11)
    pair_constants()
    query_tables()
    key_tables(1)
    pair_bias(1)
    wait(12, 13, 14, 15)
    cond_values(1)
    cond_values(2)
    attend(0, 1)
    transition(0, 1)
    project(1, 1)

    for copy in remote[0:6]:
        copy.wait_recv()
    key_tables(0)
    pair_bias(0)
    for copy in remote[6:8]:
        copy.wait_recv()
    attend(0, 0)
    transition(0, 0)
    project(1, 0)
    send_kv(1)
    for layer in (1, 2):
        attend(layer, 1)
        transition(layer, 1)
        if layer == 1:
            project(2, 1)
        for copy in remote[6 + 2 * layer : 8 + 2 * layer]:
            copy.wait_recv()
        attend(layer, 0)
        transition(layer, 0)
        if layer == 1:
            project(2, 0)
            send_kv(2)
    for copy in remote:
        copy.wait_send()


def local(*args):
    args = list(args)
    args[3] = args[3].reshape(1, A)
    vmem = pltpu.VMEM
    return pl.pallas_call(
        kernel,
        out_shape=jax.ShapeDtypeStruct((S, A, C), BF16),
        in_specs=[pl.BlockSpec(memory_space=pl.ANY)] * 15,
        out_specs=pl.BlockSpec(memory_space=pltpu.VMEM),
        scratch_shapes=[
            vmem((S, A, C), BF16),
            vmem((EXT, C), BF16),
            vmem((3, 3 * A), F32),
            vmem((1, 3 * A), jnp.int32),
            vmem((CP, 5), F32),
            vmem((CP, 9), F32),
            vmem((2, C, CP), BF16),
            vmem((3, CP, CP), F32),
            vmem((LAYERS, HEADS, CP), F32),
            vmem((LAYERS, C, 6 * C), BF16),
            vmem((LAYERS, C, 4 * C), BF16),
            vmem((LAYERS, C), F32),
            vmem((LAYERS, C, C), BF16),
            vmem((LAYERS, C, 2 * FFH), BF16),
            vmem((LAYERS, FFH, C), BF16),
            vmem((LAYERS, 6, A, C), F32),
            vmem((2, S, 128, C), F32),
            vmem((2, S, 128, C), BF16),
            vmem((2, S, 128, C), F32),
            vmem((2, S, 128, C), BF16),
            vmem((LAYERS, S, EXT, 2 * C), BF16),
            vmem((LAYERS, 2, 4, HEADS * QW, C), F32),
            vmem((256, 256), BF16),
            vmem((256, C), BF16),
            vmem((3, 256, 256), BF16),
            vmem((192, 256), BF16),
            vmem((A, C), F32),
            vmem((A, C), BF16),
            vmem((2, 4, 8, C), F32),
            vmem((2, 4, 32, C), BF16),
            pltpu.SemaphoreType.DMA((16,)),
            pltpu.SemaphoreType.DMA((12,)),
            pltpu.SemaphoreType.DMA((12,)),
        ],
        compiler_params=pltpu.CompilerParams(collective_id=0, has_side_effects=True),
        name="atom_layers",
    )(*args)


def solution(mesh):
    in_specs = (P("sample", "atom", None), P("atom", None), P(None, "atom"), P("atom")) + (P(),) * 11
    return jax.shard_map(
        local, mesh=mesh, in_specs=in_specs, out_specs=P("sample", "atom", None), check_vma=False
    )
```
